32 devices in a mesh: ctx: 16 (over z, x, core), head: 2 (over y).
Axes of the slice: x: 2, y: 2, z: 4, core: 2. Of those that a mesh axis runs over, the one named last changes fastest.
Arguments:
- queries: bfloat16 [2, 16384, 128], P('head', 'ctx'), may hold values from -12 to 12
- key_rows: bfloat16 [2, 16384, 128], P('head', 'ctx'), may hold values from -12 to 12
- value_rows: bfloat16 [2, 16384, 128], P('head', 'ctx'), may hold values from -6 to 6
- cluster_ids: int32 [2, 16384, 1], P('head', 'ctx'), may hold values from 0 to 31; in each aligned block of 1024 rows (0 to 1023, 1024 to 2047, ..., all dimensions but the last counted through in order) at most 64 rows name the same one
- out_weight: bfloat16 [256, 2048], P(None, 'head'), may hold values from -0.375 to 0.375
Outputs:
- projected: bfloat16 [16384, 2048], P('ctx', 'head')
- centroids: float32 [2, 32, 128], P('head', 'ctx')
The draws below stay inside these ranges and needn't reach their ends.
Inputs may be any that keep to these rules, and one draw needn't show every extreme that they name: `cluster_ids`: in each head, the 1024 tokens of one index of ctx name no cluster more than 64 times, a bound that some block reaches.
All inputs are finite; a program needn't handle non-finite values.
Results may differ from the reference program's by a relative error of at most 0.0054.
Values may be sent and summed in bfloat16 or wider, within the bound.
A program may use at most 64 MiB of HBM per device.

```python
import math
import jax
import jax.numpy as jnp
import numpy as np
from jax import lax

TOK_DEV = 1024
DH = 128
CAP = 1024
OUTW = 2048
HEADS = 2
CLUSTERS = 32
TOKENS = 16384
N_CTX = 16


def drawn_rows(key, salt):
    rows = jax.random.normal(jax.random.fold_in(key, salt), (HEADS, TOKENS, DH), jnp.float32)
    return jnp.clip(rows, -4.0, 4.0).astype(jnp.bfloat16)


def draw_queries(key, part):
    return drawn_rows(key, 101)


def draw_key_rows(key, part):
    return drawn_rows(key, 211)


def block_levels(stream_key, shape, split, least, largest):
    factor_of, own = 1.0, jax.random.fold_in(stream_key, 6)
    for position, shards_of in split:
        steps = jnp.exp(jax.random.uniform(jax.random.fold_in(own, position), (shards_of,), jnp.float32, least / len(split), largest / len(split)))
        factor_of = factor_of * jnp.repeat(steps, shape[position] // shards_of).reshape([-1 if axis == position else 1 for axis in range(len(shape))])
    return factor_of


def routed_block(key, own, number, rows, count, top, bound, skew):
    ranking = jax.random.permutation(key, count)
    crowded, ordinary = shares(count, rows * top, bound, skew, True), shares(count, rows * top, bound, skew, False)
    places = jnp.arange(count)

    def named(lengths, turn):
        used = int((lengths > 0).sum())
        fixed = max(1, used // 4)
        shifted = fixed + (places - fixed + turn * (used - fixed)) % max(1, count - fixed)
        return jnp.zeros((count,), jnp.int32).at[ranking[jnp.where(places < fixed, places, shifted)]].set(jnp.asarray(lengths, jnp.int32))

    lengths = jnp.where(number % 4 == 0, named(crowded, number // 4), named(ordinary, number - number // 4 - 1))
    mixed = jax.random.permutation(jax.random.fold_in(own, 3), count)
    giver, receiver = mixed[0:count // 2 * 2:2], mixed[1:count // 2 * 2:2]
    slack = jnp.minimum(lengths[giver] - 1, bound - lengths[receiver]) // 2
    slack = jnp.where((giver == ranking[0]) | (receiver == ranking[0]) | (lengths[receiver] == 0), 0, jnp.maximum(slack, 0))
    shifted = jax.random.randint(jax.random.fold_in(own, 4), (count // 2,), 0, 1 << 20) % (slack + 1)
    lengths = lengths.at[giver].add(-shifted).at[receiver].add(shifted)
    items = jnp.searchsorted(jnp.cumsum(lengths), jnp.arange(rows * top), side="right").astype(jnp.int32)
    table = items.reshape(top, rows).T
    table = table[jax.random.permutation(jax.random.fold_in(own, 1), rows)]
    turn = jax.random.randint(jax.random.fold_in(own, 2), (rows, 1), 0, top)
    return jnp.take_along_axis(table, (jnp.arange(top)[None, :] + turn) % top, axis=1)


def shares(number_of, total, most, lean, full):
    loads = [(1 << 20) // math.isqrt(rank ** lean) + 1 for rank in range(1, number_of + 1)]
    largest = most if full else min(most, max(-(-total // number_of), total * loads[0] // sum(loads)))
    least = 1 if total - largest >= number_of - 1 else 0
    given, rest = [largest] + [least] * (number_of - 1), total - largest - least * (number_of - 1)
    while rest > 0:
        candidates = [i for i in range(1, number_of) if given[i] < largest] or [i for i in range(1, number_of) if given[i] < most]
        mass, left = sum([loads[i] for i in candidates]), rest
        for i in candidates:
            addition = min(most - given[i], max(1, left * loads[i] // mass), rest)
            given[i] = given[i] + addition
            rest = rest - addition
    return np.array(given)


def normal_values(own_key, shape, deviation, bound, split=(), held_as=jnp.bfloat16):
    array = deviation * jax.random.normal(own_key, shape, jnp.float32)
    if split:
        array = array * block_levels(own_key, shape, split, -0.22, 0.18)
    return jnp.clip(array, -bound, bound).astype(held_as)


def setup_inputs(seed: int = 0) -> dict:
    splits = jax.random.split(jax.random.key(seed), 6)
    queries = draw_queries(jax.random.fold_in(splits[5], 71), 0)
    key_rows = draw_key_rows(jax.random.fold_in(splits[5], 71), 0)
    value_rows = normal_values(splits[2], (HEADS, TOKENS, DH), 1.0, 6.0, ((0, 2), (1, 16)))
    cluster_ids_keys = jax.random.split(jax.random.fold_in(splits[3], 1), HEADS * TOKENS // TOK_DEV)
    cluster_ids_turns = jax.random.permutation(jax.random.fold_in(splits[3], 3), HEADS * TOKENS // TOK_DEV)
    cluster_ids = jax.vmap(lambda own, number: routed_block(jax.random.fold_in(splits[3], 2), own, number, TOK_DEV, CLUSTERS, 1, CAP // N_CTX, 2))(cluster_ids_keys, cluster_ids_turns).reshape((HEADS, TOKENS, 1))
    out_weight = normal_values(splits[4], (HEADS * DH, OUTW), (HEADS * DH) ** -0.5, 0.375, ((1, 2),))
    return {"queries": queries, "key_rows": key_rows, "value_rows": value_rows, "cluster_ids": cluster_ids, "out_weight": out_weight}


norm_eps = 1e-06

def ranks_of(group):
    length = group.shape[0]
    block = math.gcd(512, length)
    columns = jnp.arange(length, dtype=jnp.int32)

    def block_ranks(start):
        mine = lax.dynamic_slice_in_dim(group, start, block)
        positions = start + jnp.arange(block, dtype=jnp.int32)
        earlier = (mine[:, None] == group[None, :]) & (columns[None, :] < positions[:, None])
        return lax.optimization_barrier(jnp.sum(earlier.astype(jnp.int32), axis=1))
    starts = jnp.arange(length // block, dtype=jnp.int32) * block
    return lax.map(block_ranks, starts).reshape(length)

def unit_rows(values):
    values = values.astype(jnp.float32)
    return values * lax.rsqrt(lax.optimization_barrier(jnp.mean(values * values, axis=-1, keepdims=True)) + norm_eps)

def cluster_attention(block_q, block_k, block_v, valid):
    length = block_q.shape[0]
    scores = lax.dot_general(block_q, block_k, (((1,), (1,)), ((), ())), preferred_element_type=jnp.float32)
    scores = scores * jnp.float32(block_q.shape[1] ** (-0.5))
    slots = jnp.arange(length, dtype=jnp.int32)
    allowed = (slots[None, :] <= slots[:, None]) & ((valid[None, :] > 0) | (slots[None, :] == slots[:, None]))
    scores = jnp.where(allowed, scores, jnp.float32(-1e+30))
    highest = lax.optimization_barrier(jnp.max(scores, axis=1, keepdims=True))
    weights = jnp.exp(scores - highest)
    total = lax.optimization_barrier(jnp.sum(weights, axis=1, keepdims=True))
    mixed = jnp.dot(weights.astype(jnp.bfloat16), block_v, preferred_element_type=jnp.float32)
    return (mixed / total).astype(jnp.bfloat16)

def head_output(head_q, head_k, head_v, group):
    tokens = group.shape[0]
    per_device = tokens // N_CTX
    send = CAP // N_CTX
    rank = lax.map(ranks_of, group.reshape(N_CTX, per_device)).reshape(tokens)
    source = jnp.arange(tokens, dtype=jnp.int32) // per_device
    where_row = (group * CAP + source * send + rank).astype(jnp.int32)
    total_rows = CLUSTERS * CAP

    def placed_rows(values):
        return jnp.zeros((total_rows, values.shape[1]), values.dtype).at[where_row].set(values)
    buffer_q = placed_rows(head_q)
    buffer_k = placed_rows(head_k)
    buffer_v = placed_rows(head_v)
    valid = jnp.zeros((total_rows,), jnp.int32).at[where_row].set(1)

    def one_cluster(index):
        start = (index * CAP).astype(jnp.int32)
        return cluster_attention(lax.dynamic_slice_in_dim(buffer_q, start, CAP), lax.dynamic_slice_in_dim(buffer_k, start, CAP), lax.dynamic_slice_in_dim(buffer_v, start, CAP), lax.dynamic_slice_in_dim(valid, start, CAP))
    attended = lax.map(one_cluster, jnp.arange(CLUSTERS, dtype=jnp.int32))
    return attended.reshape(total_rows, head_q.shape[1])[where_row]

def reference(queries, key_rows, value_rows, cluster_ids, out_weight):
    attended_all = []
    centroid_all = []
    for head in range(HEADS):
        group = cluster_ids[head, :, 0]
        attended_all.append(head_output(queries[head], key_rows[head], value_rows[head], group))
        unit = unit_rows(queries[head]) + unit_rows(key_rows[head])
        sums = jax.ops.segment_sum(unit, group, num_segments=CLUSTERS)
        centroid_all.append(sums * lax.rsqrt(lax.optimization_barrier(jnp.mean(sums * sums, axis=-1, keepdims=True)) + norm_eps))
    joined = jnp.concatenate(attended_all, axis=1)
    joined = joined.reshape(N_CTX, TOK_DEV, HEADS * DH)

    def project_block(rows):
        return jnp.dot(rows, out_weight, preferred_element_type=jnp.float32).astype(jnp.bfloat16)
    projected = lax.map(project_block, joined).reshape(TOKENS, OUTW)
    centroids = jnp.stack(centroid_all, axis=0)
    return (projected, centroids)
```

```python
import functools

import jax
import jax.numpy as jnp
from jax import lax
from jax.experimental import pallas as pl
from jax.experimental.pallas import tpu as pltpu
from jax.sharding import PartitionSpec as P

CL_DEV = 2
CAP = 1024
EMPTY = 2.0**100
LOW = -1e30

norm_eps = 1e-06
MESH = pl.DeviceIdType.MESH


def dot_t(a, b):
    return lax.dot_general(a, b, (((1,), (1,)), ((), ())), preferred_element_type=jnp.float32)


def unit_rows(values):
    return values * lax.rsqrt(jnp.mean(values * values, axis=-1, keepdims=True) + norm_eps)


def slots_of(ids, clusters, send):
    tokens = ids.shape[1]
    step = min(256, tokens)
    names = lax.broadcasted_iota(jnp.int32, (clusters, step), 0)
    before = lax.broadcasted_iota(jnp.int32, (step, step), 0)
    after = lax.broadcasted_iota(jnp.int32, (step, step), 1)
    earlier = jnp.where(before < after, 1.0, 0.0).astype(jnp.bfloat16)
    carry = jnp.zeros((clusters, 1), jnp.float32)
    out = []
    for start in range(0, tokens, step):
        part = ids[:, start : start + step]
        named = jnp.where(names == part, 1.0, 0.0)
        count = jnp.dot(named.astype(jnp.bfloat16), earlier, preferred_element_type=jnp.float32)
        rank = jnp.sum(named * (count + carry), axis=0, keepdims=True)
        carry = carry + jnp.sum(named, axis=1, keepdims=True)
        out.append(part * send + rank.astype(jnp.int32))
    return jnp.concatenate(out, axis=1)


def kernel(n, heads, send, q_hbm, k_hbm, v_hbm, ids_ref, joined_ref, cent_ref,
           rows, msg, recv, att, back, keys, bias, in_sem, f_send, f_recv, b_send, b_recv, h_send, h_recv):
    tokens, width = q_hbm.shape[1], q_hbm.shape[2]
    pack = CL_DEV * send
    clusters = CL_DEV * n
    me = lax.axis_index("ctx")
    head = lax.axis_index("head")

    loads = []
    for i, ref in enumerate((q_hbm, k_hbm, v_hbm)):
        load = pltpu.make_async_copy(ref.at[0], rows.at[:, i * width : (i + 1) * width], in_sem.at[i])
        load.start()
        loads.append(load)

    barrier = pltpu.get_barrier_semaphore()

    def greet(i, carry):
        pl.semaphore_signal(barrier, inc=1, device_id=(lax.rem(me + i, n), head), device_id_type=MESH)
        return carry

    lax.fori_loop(1, n, greet, 0)
    for i in range(1, heads):
        pl.semaphore_signal(barrier, inc=1, device_id=(me, lax.rem(head + i, heads)), device_id_type=MESH)

    slot_row = slots_of(ids_ref[...], clusters, send)
    slot_col = jnp.transpose(jnp.broadcast_to(slot_row, (128, tokens)))
    rows[:, 3 * width :] = jnp.ones((tokens, width), jnp.bfloat16)
    for load in loads:
        load.wait()

    chunk = max(128, pack)
    peers = chunk // pack
    chunks = n // peers
    chunk_iota = lax.broadcasted_iota(jnp.int32, (chunk, tokens), 0)
    mine = me // peers

    def fill(c):
        place = jnp.where(chunk_iota + c * chunk == slot_row, 1.0, 0.0).astype(jnp.bfloat16)
        placed = jnp.dot(place, rows[...], preferred_element_type=jnp.float32)
        held = placed[:, 3 * width :]
        part = jnp.concatenate(
            [
                placed[:, :width],
                jnp.where(held > 0.5, placed[:, width : 2 * width], EMPTY),
                placed[:, 2 * width : 3 * width],
            ],
            axis=1,
        ).astype(jnp.bfloat16)
        msg[pl.ds(c * peers, peers)] = part.reshape(peers, pack, 3 * width)

    def forward(d):
        return pltpu.make_async_remote_copy(
            src_ref=msg.at[d], dst_ref=recv.at[me], send_sem=f_send.at[d], recv_sem=f_recv.at[me],
            device_id=(d, head), device_id_type=MESH)

    def ship(c):
        for i in range(peers):
            d = c * peers + i

            @pl.when(d != me)
            def _():
                forward(d).start()

    half = chunks // 2
    order = lambda i: lax.rem(mine + half + i, chunks)
    fill(order(0))
    pl.semaphore_wait(barrier, n - 1 + heads - 1)

    def dispatch(i, carry):
        fill(order(i))
        ship(order(i - 1))
        return carry

    lax.fori_loop(1, chunks, dispatch, 0)
    ship(order(chunks - 1))
    recv[me] = msg[me]

    def arrived(s):
        @pl.when(s != me)
        def _():
            pltpu.make_async_remote_copy(
                src_ref=msg.at[s], dst_ref=recv.at[s], send_sem=f_send.at[s], recv_sem=f_recv.at[s],
                device_id=(me, head), device_id_type=MESH).wait_recv()

    def returned(s):
        return pltpu.make_async_remote_copy(
            src_ref=att.at[s], dst_ref=back.at[me], send_sem=b_send.at[s], recv_sem=b_recv.at[me],
            device_id=(s, head), device_id_type=MESH)

    block = 256
    sources = block // send
    tri_r = lax.broadcasted_iota(jnp.int32, (block, block), 0)
    tri_c = lax.broadcasted_iota(jnp.int32, (block, block), 1)
    causal = jnp.where(tri_c <= tri_r, 0.0, LOW)
    ones = jnp.ones((8, width), jnp.bfloat16)
    sums = [jnp.zeros((1, width), jnp.float32) for _ in range(CL_DEV)]
    scale = jnp.float32(width ** (-0.5))

    for b in range(CAP // block):
        first, last = b * sources, (b + 1) * sources

        def wait_one(s, carry):
            arrived(s)
            return carry

        lax.fori_loop(first, last, wait_one, 0)
        span = (b + 1) * block
        for j in range(CL_DEV):
            inner = slice(j * send, (j + 1) * send)
            q = recv[first:last, inner, :width].reshape(block, width)
            k32 = recv[first:last, inner, width : 2 * width].reshape(block, width).astype(jnp.float32)
            vacant = k32 > 0.5 * EMPTY
            k32 = jnp.where(vacant, 0.0, k32)
            keys[j, b * block : span, :] = k32.astype(jnp.bfloat16)
            flags = dot_t(ones, jnp.where(vacant, 1.0, 0.0).astype(jnp.bfloat16))
            bias[j, :, b * block : span] = jnp.where(flags > 0.5, LOW, 0.0)
            unit = unit_rows(q.astype(jnp.float32)) + unit_rows(k32)
            sums[j] = sums[j] + jnp.sum(unit, axis=0, keepdims=True)
            scores = dot_t(q, keys[j, :span, :]) * scale + bias[j, 0:1, :span]
            tail = scores[:, b * block :] + causal
            scores = tail if b == 0 else jnp.concatenate([scores[:, : b * block], tail], axis=1)
            highest = jnp.max(scores, axis=1, keepdims=True)
            weights = jnp.exp(scores - highest)
            total = jnp.sum(weights, axis=1, keepdims=True)
            v = recv[:last, inner, 2 * width :].reshape(span, width)
            mixed = jnp.dot(weights.astype(jnp.bfloat16), v, preferred_element_type=jnp.float32)
            att[first:last, inner, :] = (mixed / total).astype(jnp.bfloat16).reshape(sources, send, width)

        def give_one(s, carry):
            @pl.when(s != me)
            def _():
                returned(s).start()

            return carry

        lax.fori_loop(first, last, give_one, 0)

    for j in range(CL_DEV):
        mean = jnp.mean(sums[j] * sums[j], axis=-1, keepdims=True)
        cent_ref[j : j + 1, :] = sums[j] * lax.rsqrt(mean + norm_eps)
    back[me] = att[me]

    slots = CL_DEV * CAP
    step = 256
    group = step // pack
    lanes = lax.broadcasted_iota(jnp.int32, (tokens, 128), 1)
    got = jnp.zeros((tokens, width), jnp.float32)
    for c in range(slots // step):

        def wait_back(s, carry):
            @pl.when(s != me)
            def _():
                pltpu.make_async_remote_copy(
                    src_ref=att.at[s], dst_ref=back.at[s], send_sem=b_send.at[s], recv_sem=b_recv.at[s],
                    device_id=(me, head), device_id_type=MESH).wait_recv()

            return carry

        lax.fori_loop(c * group, (c + 1) * group, wait_back, 0)
        pick = jnp.concatenate(
            [jnp.where(slot_col == lanes + (c * step + i), 1.0, 0.0) for i in range(0, step, 128)], axis=1
        ).astype(jnp.bfloat16)
        piece = back[c * group : (c + 1) * group].reshape(step, width)
        got = got + jnp.dot(pick, piece, preferred_element_type=jnp.float32)

    own = pl.ds(pl.multiple_of(head * width, width), width)
    joined_ref[:, own] = got.astype(jnp.bfloat16)

    def share(i):
        return pltpu.make_async_remote_copy(
            src_ref=joined_ref.at[:, own], dst_ref=joined_ref.at[:, own],
            send_sem=h_send.at[i - 1], recv_sem=h_recv.at[i - 1],
            device_id=(me, lax.rem(head + i, heads)), device_id_type=MESH)

    for i in range(1, heads):
        share(i).start()

    def sent(i, carry):
        d = lax.rem(me + i, n)
        forward(d).wait_send()
        returned(d).wait_send()
        return carry

    lax.fori_loop(1, n, sent, 0)
    for i in range(1, heads):
        share(i).wait_send()
        other = pl.ds(pl.multiple_of(lax.rem(head + heads - i, heads) * width, width), width)
        pltpu.make_async_remote_copy(
            src_ref=joined_ref.at[:, other], dst_ref=joined_ref.at[:, other],
            send_sem=h_send.at[i - 1], recv_sem=h_recv.at[i - 1],
            device_id=(me, head), device_id_type=MESH).wait_recv()


def shards(n, heads, queries, key_rows, value_rows, cluster_ids, out_weight):
    tokens, width = queries.shape[1], queries.shape[2]
    send = CAP // n
    pack = CL_DEV * send
    bf16, f32 = jnp.bfloat16, jnp.float32
    dma = pltpu.SemaphoreType.DMA
    joined, centroids = pl.pallas_call(
        functools.partial(kernel, n, heads, send),
        out_shape=(
            jax.ShapeDtypeStruct((tokens, heads * width), bf16),
            jax.ShapeDtypeStruct((CL_DEV, width), f32),
        ),
        in_specs=[pl.BlockSpec(memory_space=pl.ANY)] * 3 + [pl.BlockSpec(memory_space=pltpu.VMEM)],
        out_specs=(pl.BlockSpec(memory_space=pltpu.VMEM), pl.BlockSpec(memory_space=pltpu.VMEM)),
        scratch_shapes=[
            pltpu.VMEM((tokens, 4 * width), bf16),
            pltpu.VMEM((n, pack, 3 * width), bf16),
            pltpu.VMEM((n, pack, 3 * width), bf16),
            pltpu.VMEM((n, pack, width), bf16),
            pltpu.VMEM((n, pack, width), bf16),
            pltpu.VMEM((CL_DEV, CAP, width), bf16),
            pltpu.VMEM((CL_DEV, 8, CAP), f32),
            dma((3,)),
            dma((n,)),
            dma((n,)),
            dma((n,)),
            dma((n,)),
            dma((max(1, heads - 1),)),
            dma((max(1, heads - 1),)),
        ],
        compiler_params=pltpu.CompilerParams(
            collective_id=0, has_side_effects=True, vmem_limit_bytes=48 * 1024 * 1024
        ),
        name="route",
    )(queries, key_rows, value_rows, cluster_ids[0, :, 0][None, :])
    projected = jnp.dot(joined, out_weight, preferred_element_type=f32).astype(bf16)
    return (projected, centroids[None])


def solution(mesh):
    in_specs = (
        P("head", "ctx", None),
        P("head", "ctx", None),
        P("head", "ctx", None),
        P("head", "ctx", None),
        P(None, "head"),
    )
    out_specs = (P("ctx", "head"), P("head", "ctx", None))
    body = functools.partial(shards, mesh.shape["ctx"], mesh.shape["head"])
    return jax.shard_map(body, mesh=mesh, in_specs=in_specs, out_specs=out_specs, check_vma=False)
```

```python
import functools

import jax
import jax.numpy as jnp
from jax import lax
from jax.experimental import pallas as pl
from jax.experimental.pallas import tpu as pltpu
from jax.sharding import PartitionSpec as P

CL_DEV = 2
CAP = 1024
QUARTERS = 4
EMPTY = 2.0**100
LOW = -1e30

norm_eps = 1e-06
MESH = pl.DeviceIdType.MESH


def dot_t(a, b):
    return lax.dot_general(a, b, (((1,), (1,)), ((), ())), preferred_element_type=jnp.float32)


def unit_rows(values):
    return values * lax.rsqrt(jnp.mean(values * values, axis=-1, keepdims=True) + norm_eps)


def slots_of(ids, clusters, send):
    tokens = ids.shape[1]
    step = min(256, tokens)
    names = lax.broadcasted_iota(jnp.int32, (clusters, step), 0)
    before = lax.broadcasted_iota(jnp.int32, (step, step), 0)
    after = lax.broadcasted_iota(jnp.int32, (step, step), 1)
    earlier = jnp.where(before < after, 1.0, 0.0).astype(jnp.bfloat16)
    carry = jnp.zeros((clusters, 1), jnp.float32)
    out = []
    for start in range(0, tokens, step):
        part = ids[:, start : start + step]
        named = jnp.where(names == part, 1.0, 0.0)
        count = jnp.dot(named.astype(jnp.bfloat16), earlier, preferred_element_type=jnp.float32)
        rank = jnp.sum(named * (count + carry), axis=0, keepdims=True)
        carry = carry + jnp.sum(named, axis=1, keepdims=True)
        out.append(part * send + rank.astype(jnp.int32))
    return jnp.concatenate(out, axis=1)


def kernel(n, heads, send, q_hbm, k_hbm, v_hbm, ids_ref, joined_ref, cent_ref,
           rows, msg, recv, att, back, keys, bias, sums, gathered,
           in_sem, f_send, f_recv, b_send, b_recv, c_send, c_recv, h_send, h_recv):
    tokens, width = q_hbm.shape[1], q_hbm.shape[2]
    clusters = CL_DEV * n
    part = n // QUARTERS
    owned = clusters // (2 * part)
    pack = owned * send
    me = lax.axis_index("ctx")
    head = lax.axis_index("head")
    zone = me // part
    spot = lax.rem(me, part)

    loads = []
    for i, ref in enumerate((q_hbm, k_hbm, v_hbm)):
        load = pltpu.make_async_copy(ref.at[0], rows.at[:, i * width : (i + 1) * width], in_sem.at[i])
        load.start()
        loads.append(load)

    barrier = pltpu.get_barrier_semaphore()

    def greet(i, carry):
        pl.semaphore_signal(barrier, inc=1, device_id=(lax.rem(me + i, n), head), device_id_type=MESH)
        return carry

    lax.fori_loop(1, n, greet, 0)
    for i in range(1, heads):
        pl.semaphore_signal(barrier, inc=1, device_id=(me, lax.rem(head + i, heads)), device_id_type=MESH)

    slot_row = slots_of(ids_ref[...], clusters, send)
    slot_col = jnp.transpose(jnp.broadcast_to(slot_row, (128, tokens)))
    rows[:, 3 * width :] = jnp.ones((tokens, width), jnp.bfloat16)
    for load in loads:
        load.wait()

    chunk = 256
    peers = chunk // pack
    chunks = part // peers
    chunk_iota = lax.broadcasted_iota(jnp.int32, (chunk, tokens), 0)

    def fill(kind, c):
        base = (kind * chunks + c) * chunk
        place = jnp.where(chunk_iota + base == slot_row, 1.0, 0.0).astype(jnp.bfloat16)
        placed = jnp.dot(place, rows[...], preferred_element_type=jnp.float32)
        held = placed[:, 3 * width :]
        new = jnp.concatenate(
            [
                placed[:, :width],
                jnp.where(held > 0.5, placed[:, width : 2 * width], EMPTY),
                placed[:, 2 * width : 3 * width],
            ],
            axis=1,
        ).astype(jnp.bfloat16)
        msg[kind, pl.ds(c * peers, peers)] = new.reshape(peers, pack, 3 * width)

    def forward(kind, spot_to, zone_to, source, whole):
        cols = slice(0, 3 * width) if whole else slice(width, 3 * width)
        d = zone_to * part + spot_to
        return pltpu.make_async_remote_copy(
            src_ref=msg.at[kind, spot_to, :, cols], dst_ref=recv.at[kind, source, :, cols],
            send_sem=f_send.at[kind, d], recv_sem=f_recv.at[kind, source],
            device_id=(d, head), device_id_type=MESH)

    def each_send(kind, i, act, local):
        @pl.when(kind == 1)
        def _():
            @pl.when(zone < 2)
            def _():
                act(forward(1, i, 2, me, False))

            @pl.when(zone == 0)
            def _():
                act(forward(1, i, 1, me, False))

            @pl.when(zone == 3)
            def _():
                act(forward(1, i, 2, me, True))

        @pl.when(kind == 0)
        def _():
            @pl.when(zone == 0)
            def _():
                act(forward(0, i, 1, me, False))

            @pl.when(zone >= 2)
            def _():
                act(forward(0, i, 1, me, True))

        @pl.when((zone < 3 - (1 - kind)) & (i != spot))
        def _():
            act(forward(kind, i, zone, me, True))

        if local:
            @pl.when((zone < 3 - (1 - kind)) & (i == spot))
            def _():
                recv[kind, me] = msg[kind, i]

    def ship(t):
        kind, c = kind_of(t), lax.rem(t, chunks)
        for p in range(peers):
            each_send(kind, c * peers + p, lambda copy: copy.start(), True)

    def kind_of(t):
        return lax.rem(1 - zone // 2 + t // chunks, 2)

    fill(kind_of(0), 0)
    pl.semaphore_wait(barrier, n - 1 + heads - 1)

    def dispatch(t, carry):
        fill(kind_of(t), lax.rem(t, chunks))
        ship(t - 1)
        return carry

    lax.fori_loop(1, 2 * chunks, dispatch, 0)
    ship(2 * chunks - 1)

    unit = unit_rows(rows[:, :width].astype(jnp.float32)) + unit_rows(rows[:, width : 2 * width].astype(jnp.float32))
    upper = unit.astype(jnp.bfloat16)
    lower = (unit - upper.astype(jnp.float32)).astype(jnp.bfloat16)
    names = lax.broadcasted_iota(jnp.int32, (clusters, tokens), 0)
    named = jnp.where(names == ids_ref[...], 1.0, 0.0).astype(jnp.bfloat16)
    local_sums = jnp.dot(named, upper, preferred_element_type=jnp.float32) + jnp.dot(
        named, lower, preferred_element_type=jnp.float32)
    sums[...] = local_sums.reshape(n, CL_DEV, width)

    def summed(d, source):
        return pltpu.make_async_remote_copy(
            src_ref=sums.at[d], dst_ref=gathered.at[source], send_sem=c_send.at[d], recv_sem=c_recv.at[source],
            device_id=(d, head), device_id_type=MESH)

    def send_sums(i, carry):
        summed(lax.rem(me + i, n), me).start()
        return carry

    gathered[me] = sums[me]
    lax.fori_loop(1, n, send_sums, 0)

    def arrived(kind, first, whole):
        def one(s, carry):
            @pl.when(s != me)
            def _():
                cols = slice(0, 3 * width) if whole else slice(width, 3 * width)
                pltpu.make_async_remote_copy(
                    src_ref=msg.at[kind, 0, :, cols], dst_ref=recv.at[kind, s, :, cols],
                    send_sem=f_send.at[kind, s], recv_sem=f_recv.at[kind, s],
                    device_id=(me, head), device_id_type=MESH).wait_recv()

            return carry

        lax.fori_loop(first * part, (first + 1) * part, one, 0)

    def returned(kind, d):
        return pltpu.make_async_remote_copy(
            src_ref=att.at[kind, d], dst_ref=back.at[kind, spot], send_sem=b_send.at[kind, d],
            recv_sem=b_recv.at[kind, spot], device_id=(d, head), device_id_type=MESH)

    block = part * send
    tri_r = lax.broadcasted_iota(jnp.int32, (block, block), 0)
    tri_c = lax.broadcasted_iota(jnp.int32, (block, block), 1)
    causal = jnp.where(tri_c <= tri_r, 0.0, LOW)
    ones = jnp.ones((8, width), jnp.bfloat16)
    scale = jnp.float32(width ** (-0.5))

    def prepare(kind, p, j):
        inner = pl.ds(pl.multiple_of(j * send, send), send)
        lanes = slice(p * block, (p + 1) * block)
        k32 = recv[kind, p * part : (p + 1) * part, inner, width : 2 * width].reshape(block, width).astype(jnp.float32)
        vacant = k32 > 0.5 * EMPTY
        keys[kind, j, lanes, :] = jnp.where(vacant, 0.0, k32).astype(jnp.bfloat16)
        flags = dot_t(ones, jnp.where(vacant, 1.0, 0.0).astype(jnp.bfloat16))
        bias[kind, j, :, lanes] = jnp.where(flags > 0.5, LOW, 0.0)

    def attend(kind, p, j):
        inner = pl.ds(pl.multiple_of(j * send, send), send)
        first, last, span = p * part, (p + 1) * part, (p + 1) * block
        q = recv[kind, first:last, inner, :width].reshape(block, width)
        scores = dot_t(q, keys[kind, j, :span, :]) * scale + bias[kind, j, 0:1, :span]
        tail = scores[:, p * block :] + causal
        scores = tail if p == 0 else jnp.concatenate([scores[:, : p * block], tail], axis=1)
        highest = jnp.max(scores, axis=1, keepdims=True)
        weights = jnp.exp(scores - highest)
        total = jnp.sum(weights, axis=1, keepdims=True)
        v = recv[kind, :last, inner, 2 * width :].reshape(span, width)
        mixed = jnp.dot(weights.astype(jnp.bfloat16), v, preferred_element_type=jnp.float32)
        att[kind, first:last, inner, :] = (mixed / total).astype(jnp.bfloat16).reshape(part, send, width)

    def paired(act):
        def two(jj, carry):
            act(2 * jj)
            act(2 * jj + 1)
            return carry

        lax.fori_loop(0, owned // 2, two, 0)

    def ready(kind, p, whole):
        arrived(kind, p, whole)
        paired(lambda j: prepare(kind, p, j))

    def answer(kind, p):
        paired(lambda j: attend(kind, p, j))

        def one(s, carry):
            @pl.when(s != me)
            def _():
                returned(kind, s).start()

            @pl.when(s == me)
            def _():
                back[kind, spot] = att[kind, s]

            return carry

        lax.fori_loop(p * part, (p + 1) * part, one, 0)

    @pl.when(zone == 0)
    def _():
        for kind in (1, 0):
            ready(kind, 0, True)
            answer(kind, 0)

    @pl.when(zone == 1)
    def _():
        for kind in (1, 0):
            ready(kind, 0, False)
            ready(kind, 1, True)
            answer(kind, 1)
        for p in (2, 3):
            ready(0, p, True)
            answer(0, p)

    @pl.when(zone == 2)
    def _():
        ready(1, 0, False)
        ready(1, 1, False)
        for p in (2, 3):
            ready(1, p, True)
            answer(1, p)

    slots = clusters * send
    lanes = lax.broadcasted_iota(jnp.int32, (tokens, 128), 1)
    got = jnp.zeros((tokens, width), jnp.float32)
    for c in range(slots // chunk):
        kind, start = c // chunks, (c % chunks) * peers
        giver = jnp.minimum(zone, kind + 1) * part

        def wait_back(s, carry):
            @pl.when(giver + s != me)
            def _():
                pltpu.make_async_remote_copy(
                    src_ref=att.at[kind, s], dst_ref=back.at[kind, s], send_sem=b_send.at[kind, s],
                    recv_sem=b_recv.at[kind, s], device_id=(me, head), device_id_type=MESH).wait_recv()

            return carry

        lax.fori_loop(start, start + peers, wait_back, 0)
        pick = jnp.concatenate(
            [jnp.where(slot_col == lanes + (c * chunk + i), 1.0, 0.0) for i in range(0, chunk, 128)], axis=1
        ).astype(jnp.bfloat16)
        piece = back[kind, start : start + peers].reshape(chunk, width)
        got = got + jnp.dot(pick, piece, preferred_element_type=jnp.float32)

    own = pl.ds(pl.multiple_of(head * width, width), width)
    joined_ref[:, own] = got.astype(jnp.bfloat16)

    def share(i):
        return pltpu.make_async_remote_copy(
            src_ref=joined_ref.at[:, own], dst_ref=joined_ref.at[:, own],
            send_sem=h_send.at[i - 1], recv_sem=h_recv.at[i - 1],
            device_id=(me, lax.rem(head + i, heads)), device_id_type=MESH)

    for i in range(1, heads):
        share(i).start()

    def finish(i, carry):
        s = lax.rem(me + i, n)
        summed(s, s).wait_recv()
        summed(s, me).wait_send()
        return carry

    lax.fori_loop(1, n, finish, 0)
    totals = jnp.sum(gathered[...], axis=0)
    mean = jnp.mean(totals * totals, axis=-1, keepdims=True)
    cent_ref[...] = totals * lax.rsqrt(mean + norm_eps)

    def settle(i, carry):
        each_send(0, i, lambda copy: copy.wait_send(), False)
        each_send(1, i, lambda copy: copy.wait_send(), False)
        return carry

    lax.fori_loop(0, part, settle, 0)

    def given(kind, p):
        def one(s, carry):
            @pl.when(s != me)
            def _():
                returned(kind, s).wait_send()

            return carry

        lax.fori_loop(p * part, (p + 1) * part, one, 0)

    @pl.when(zone == 0)
    def _():
        given(1, 0)
        given(0, 0)

    @pl.when(zone == 1)
    def _():
        given(1, 1)
        for p in (1, 2, 3):
            given(0, p)

    @pl.when(zone == 2)
    def _():
        for p in (2, 3):
            given(1, p)

    for i in range(1, heads):
        share(i).wait_send()
        other = pl.ds(pl.multiple_of(lax.rem(head + heads - i, heads) * width, width), width)
        pltpu.make_async_remote_copy(
            src_ref=joined_ref.at[:, other], dst_ref=joined_ref.at[:, other],
            send_sem=h_send.at[i - 1], recv_sem=h_recv.at[i - 1],
            device_id=(me, head), device_id_type=MESH).wait_recv()


def shards(n, heads, queries, key_rows, value_rows, cluster_ids, out_weight):
    tokens, width = queries.shape[1], queries.shape[2]
    send = CAP // n
    part = n // QUARTERS
    owned = CL_DEV * n // (2 * part)
    pack = owned * send
    bf16, f32 = jnp.bfloat16, jnp.float32
    dma = pltpu.SemaphoreType.DMA
    joined, centroids = pl.pallas_call(
        functools.partial(kernel, n, heads, send),
        out_shape=(
            jax.ShapeDtypeStruct((tokens, heads * width), bf16),
            jax.ShapeDtypeStruct((CL_DEV, width), f32),
        ),
        in_specs=[pl.BlockSpec(memory_space=pl.ANY)] * 3 + [pl.BlockSpec(memory_space=pltpu.VMEM)],
        out_specs=(pl.BlockSpec(memory_space=pltpu.VMEM), pl.BlockSpec(memory_space=pltpu.VMEM)),
        scratch_shapes=[
            pltpu.VMEM((tokens, 4 * width), bf16),
            pltpu.VMEM((2, part, pack, 3 * width), bf16),
            pltpu.VMEM((2, n, pack, 3 * width), bf16),
            pltpu.VMEM((2, n, pack, width), bf16),
            pltpu.VMEM((2, part, pack, width), bf16),
            pltpu.VMEM((2, owned, CAP, width), bf16),
            pltpu.VMEM((2, owned, 8, CAP), f32),
            pltpu.VMEM((n, CL_DEV, width), f32),
            pltpu.VMEM((n, CL_DEV, width), f32),
            dma((3,)),
            dma((2, n)),
            dma((2, n)),
            dma((2, n)),
            dma((2, part)),
            dma((n,)),
            dma((n,)),
            dma((max(1, heads - 1),)),
            dma((max(1, heads - 1),)),
        ],
        compiler_params=pltpu.CompilerParams(
            collective_id=0, has_side_effects=True, vmem_limit_bytes=60 * 1024 * 1024
        ),
        name="route",
    )(queries, key_rows, value_rows, cluster_ids[0, :, 0][None, :])
    projected = jnp.dot(joined, out_weight, preferred_element_type=f32).astype(bf16)
    return (projected, centroids[None])


def solution(mesh):
    in_specs = (
        P("head", "ctx", None),
        P("head", "ctx", None),
        P("head", "ctx", None),
        P("head", "ctx", None),
        P(None, "head"),
    )
    out_specs = (P("ctx", "head"), P("head", "ctx", None))
    body = functools.partial(shards, mesh.shape["ctx"], mesh.shape["head"])
    return jax.shard_map(body, mesh=mesh, in_specs=in_specs, out_specs=out_specs, check_vma=False)
```

```python
import functools

import jax
import jax.numpy as jnp
from jax import lax
from jax.experimental import pallas as pl
from jax.experimental.pallas import tpu as pltpu
from jax.sharding import PartitionSpec as P

CL_DEV = 2
CAP = 1024
QUARTERS = 4
EMPTY = 2.0**100
LOW = -1e30

norm_eps = 1e-06
MESH = pl.DeviceIdType.MESH


def dot_t(a, b):
    return lax.dot_general(a, b, (((1,), (1,)), ((), ())), preferred_element_type=jnp.float32)


def unit_rows(values):
    return values * lax.rsqrt(jnp.mean(values * values, axis=-1, keepdims=True) + norm_eps)


def slots_of(ids, clusters, send):
    tokens = ids.shape[1]
    step = min(256, tokens)
    names = lax.broadcasted_iota(jnp.int32, (clusters, step), 0)
    before = lax.broadcasted_iota(jnp.int32, (step, step), 0)
    after = lax.broadcasted_iota(jnp.int32, (step, step), 1)
    earlier = jnp.where(before < after, 1.0, 0.0).astype(jnp.bfloat16)
    carry = jnp.zeros((clusters, 1), jnp.float32)
    out = []
    for start in range(0, tokens, step):
        part = ids[:, start : start + step]
        named = jnp.where(names == part, 1.0, 0.0)
        count = jnp.dot(named.astype(jnp.bfloat16), earlier, preferred_element_type=jnp.float32)
        rank = jnp.sum(named * (count + carry), axis=0, keepdims=True)
        carry = carry + jnp.sum(named, axis=1, keepdims=True)
        out.append(part * send + rank.astype(jnp.int32))
    return jnp.concatenate(out, axis=1)


def kernel(n, heads, send, q_hbm, k_hbm, v_hbm, ids_ref, joined_ref, cent_ref,
           rows, msg, recv, att, back, others, keys, bias, idx, cols,
           in_sem, f_send, f_recv, b_send, b_recv, h_send, h_recv, i_send, i_recv):
    tokens, width = q_hbm.shape[1], q_hbm.shape[2]
    clusters = CL_DEV * n
    part = n // QUARTERS
    block = part * send
    me = lax.axis_index("ctx")
    head = lax.axis_index("head")
    zone = me // part

    loads = []
    for i, ref in enumerate((q_hbm, k_hbm, v_hbm)):
        load = pltpu.make_async_copy(ref.at[0], rows.at[:, i * width : (i + 1) * width], in_sem.at[i])
        load.start()
        loads.append(load)

    barrier = pltpu.get_barrier_semaphore()

    def greet(i, carry):
        pl.semaphore_signal(barrier, inc=1, device_id=(lax.rem(me + i, n), head), device_id_type=MESH)
        return carry

    lax.fori_loop(1, n, greet, 0)
    for i in range(1, heads):
        pl.semaphore_signal(barrier, inc=1, device_id=(me, lax.rem(head + i, heads)), device_id_type=MESH)

    def column(slot_row):
        return jnp.transpose(jnp.broadcast_to(slot_row, (128, tokens)))

    slot_row = slots_of(ids_ref[...], clusters, send)
    cols[0] = column(slot_row)
    rows[:, 3 * width :] = jnp.ones((tokens, width), jnp.bfloat16)
    for load in loads:
        load.wait()

    place_r = lax.broadcasted_iota(jnp.int32, (block, tokens), 0)
    place_r = place_r + (place_r // send) * ((CL_DEV - 1) * send)

    def fill(j, z):
        base = (z * part * CL_DEV + j) * send
        place = jnp.where(place_r + base == slot_row, 1.0, 0.0).astype(jnp.bfloat16)
        placed = jnp.dot(place, rows[...], preferred_element_type=jnp.float32)
        held = placed[:, 3 * width :]
        new = jnp.concatenate(
            [
                placed[:, :width],
                jnp.where(held > 0.5, placed[:, width : 2 * width], EMPTY),
                placed[:, 2 * width : 3 * width],
            ],
            axis=1,
        ).astype(jnp.bfloat16)
        msg[j, pl.ds(z * part, part)] = new.reshape(part, send, 3 * width)

    def forward(j, d, source):
        return pltpu.make_async_remote_copy(
            src_ref=msg.at[j, d], dst_ref=recv.at[j, source], send_sem=f_send.at[j, d], recv_sem=f_recv.at[j, source],
            device_id=(d, head), device_id_type=MESH)

    def ship(j, z):
        def one(i, carry):
            d = z * part + lax.rem(me + i, part)

            @pl.when(d != me)
            def _():
                forward(j, d, me).start()

            return carry

        lax.fori_loop(0, part, one, 0)

    def turn(t):
        return t // QUARTERS, lax.rem(zone + QUARTERS // 2 + lax.rem(t, QUARTERS), QUARTERS)

    def told(i):
        return pltpu.make_async_remote_copy(
            src_ref=ids_ref, dst_ref=idx.at[i - 1], send_sem=i_send.at[i - 1], recv_sem=i_recv.at[i - 1],
            device_id=(me, lax.rem(head + i, heads)), device_id_type=MESH)

    fill(*turn(0))
    pl.semaphore_wait(barrier, n - 1 + heads - 1)

    def dispatch(t, carry):
        fill(*turn(t))
        ship(*turn(t - 1))
        return carry

    steps = CL_DEV * QUARTERS
    lax.fori_loop(1, steps, dispatch, 0)
    ship(*turn(steps - 1))
    for j in range(CL_DEV):
        recv[j, me] = msg[j, me]
    for i in range(1, heads):
        told(i).start()
    for i in range(1, heads):
        told(i).wait_recv()
        cols[i] = column(slots_of(idx[i - 1], clusters, send))

    def arrived(j, z):
        def one(s, carry):
            @pl.when(s != me)
            def _():
                forward(j, s, s).wait_recv()

            return carry

        lax.fori_loop(z * part, (z + 1) * part, one, 0)

    def returned(j, s, owner):
        return pltpu.make_async_remote_copy(
            src_ref=att.at[j, s], dst_ref=back.at[j, owner], send_sem=b_send.at[j, s], recv_sem=b_recv.at[j, owner],
            device_id=(s, head), device_id_type=MESH)

    tri_r = lax.broadcasted_iota(jnp.int32, (block, block), 0)
    tri_c = lax.broadcasted_iota(jnp.int32, (block, block), 1)
    causal = jnp.where(tri_c <= tri_r, 0.0, LOW)
    ones = jnp.ones((8, width), jnp.bfloat16)
    scale = jnp.float32(width ** (-0.5))

    for j in range(CL_DEV):
        sums = jnp.zeros((1, width), jnp.float32)
        for b in range(QUARTERS):
            first, last, span = b * part, (b + 1) * part, (b + 1) * block
            arrived(j, b)
            q = recv[j, first:last, :, :width].reshape(block, width)
            k32 = recv[j, first:last, :, width : 2 * width].reshape(block, width).astype(jnp.float32)
            vacant = k32 > 0.5 * EMPTY
            k32 = jnp.where(vacant, 0.0, k32)
            keys[b * block : span, :] = k32.astype(jnp.bfloat16)
            flags = dot_t(ones, jnp.where(vacant, 1.0, 0.0).astype(jnp.bfloat16))
            bias[:, b * block : span] = jnp.where(flags > 0.5, LOW, 0.0)
            scores = dot_t(q, keys[:span, :]) * scale + bias[0:1, :span]
            tail = scores[:, b * block :] + causal
            scores = tail if b == 0 else jnp.concatenate([scores[:, : b * block], tail], axis=1)
            highest = jnp.max(scores, axis=1, keepdims=True)
            weights = jnp.exp(scores - highest)
            total = jnp.sum(weights, axis=1, keepdims=True)
            v = recv[j, :last, :, 2 * width :].reshape(span, width)
            mixed = jnp.dot(weights.astype(jnp.bfloat16), v, preferred_element_type=jnp.float32)
            att[j, first:last] = (mixed / total).astype(jnp.bfloat16).reshape(part, send, width)
            unit = unit_rows(q.astype(jnp.float32)) + unit_rows(k32)
            sums = sums + jnp.sum(unit, axis=0, keepdims=True)

            def give(s, carry):
                @pl.when(s != me)
                def _():
                    returned(j, s, me).start()

                return carry

            lax.fori_loop(first, last, give, 0)
        back[j, me] = att[j, me]
        mean = jnp.mean(sums * sums, axis=-1, keepdims=True)
        cent_ref[j : j + 1, :] = sums * lax.rsqrt(mean + norm_eps)

    lanes = lax.broadcasted_iota(jnp.int32, (tokens, block), 1)
    lanes = lanes + (lanes // send) * ((CL_DEV - 1) * send)

    def gather(got, which, j, b, piece):
        column_slots = cols[which]
        wide = column_slots if block == 128 else jnp.concatenate([column_slots] * (block // 128), axis=1)
        pick = jnp.where(wide == lanes + (b * part * CL_DEV + j) * send, 1.0, 0.0).astype(jnp.bfloat16)
        return got + jnp.dot(pick, piece.reshape(block, width), preferred_element_type=jnp.float32)

    def passed(i, j, b):
        rows_of = slice(b * part, (b + 1) * part)
        return pltpu.make_async_remote_copy(
            src_ref=back.at[j, rows_of], dst_ref=others.at[i - 1, j, rows_of],
            send_sem=h_send.at[i - 1, j, b], recv_sem=h_recv.at[i - 1, j, b],
            device_id=(me, lax.rem(head + i, heads)), device_id_type=MESH)

    pieces = [(j, b) for j in range(CL_DEV) for b in range(QUARTERS)]
    got = jnp.zeros((tokens, width), jnp.float32)
    for j, b in pieces:

        def wait_back(s, carry):
            @pl.when(s != me)
            def _():
                returned(j, s, s).wait_recv()

            return carry

        lax.fori_loop(b * part, (b + 1) * part, wait_back, 0)
        for i in range(1, heads):
            passed(i, j, b).start()
        got = gather(got, 0, j, b, back[j, b * part : (b + 1) * part])
    joined_ref[:, pl.ds(pl.multiple_of(head * width, width), width)] = got.astype(jnp.bfloat16)

    for i in range(1, heads):
        got = jnp.zeros((tokens, width), jnp.float32)
        for j, b in pieces:
            passed(i, j, b).wait_recv()
            got = gather(got, i, j, b, others[i - 1, j, b * part : (b + 1) * part])
        source = lax.rem(head + heads - i, heads)
        joined_ref[:, pl.ds(pl.multiple_of(source * width, width), width)] = got.astype(jnp.bfloat16)

    def settle(i, carry):
        d = lax.rem(me + i, n)
        for j in range(CL_DEV):
            forward(j, d, me).wait_send()
            returned(j, d, me).wait_send()
        return carry

    lax.fori_loop(1, n, settle, 0)
    for i in range(1, heads):
        told(i).wait_send()
        for j, b in pieces:
            passed(i, j, b).wait_send()


def shards(n, heads, queries, key_rows, value_rows, cluster_ids, out_weight):
    tokens, width = queries.shape[1], queries.shape[2]
    send = CAP // n
    bf16, f32 = jnp.bfloat16, jnp.float32
    dma = pltpu.SemaphoreType.DMA
    joined, centroids = pl.pallas_call(
        functools.partial(kernel, n, heads, send),
        out_shape=(
            jax.ShapeDtypeStruct((tokens, heads * width), bf16),
            jax.ShapeDtypeStruct((CL_DEV, width), f32),
        ),
        in_specs=[pl.BlockSpec(memory_space=pltpu.HBM)] * 3 + [pl.BlockSpec(memory_space=pltpu.VMEM)],
        out_specs=(pl.BlockSpec(memory_space=pltpu.VMEM), pl.BlockSpec(memory_space=pltpu.VMEM)),
        scratch_shapes=[
            pltpu.VMEM((tokens, 4 * width), bf16),
            pltpu.VMEM((CL_DEV, n, send, 3 * width), bf16),
            pltpu.VMEM((CL_DEV, n, send, 3 * width), bf16),
            pltpu.VMEM((CL_DEV, n, send, width), bf16),
            pltpu.VMEM((CL_DEV, n, send, width), bf16),
            pltpu.VMEM((max(1, heads - 1), CL_DEV, n, send, width), bf16),
            pltpu.VMEM((CAP, width), bf16),
            pltpu.VMEM((8, CAP), f32),
            pltpu.VMEM((max(1, heads - 1), 1, tokens), jnp.int32),
            pltpu.VMEM((heads, tokens, 128), jnp.int32),
            dma((3,)),
            dma((CL_DEV, n)),
            dma((CL_DEV, n)),
            dma((CL_DEV, n)),
            dma((CL_DEV, n)),
            dma((max(1, heads - 1), CL_DEV, QUARTERS)),
            dma((max(1, heads - 1), CL_DEV, QUARTERS)),
            dma((max(1, heads - 1),)),
            dma((max(1, heads - 1),)),
        ],
        compiler_params=pltpu.CompilerParams(
            collective_id=0, has_side_effects=True, vmem_limit_bytes=60000000
        ),
        name="route",
    )(queries, key_rows, value_rows, cluster_ids[0, :, 0][None, :])
    projected = jnp.dot(joined, out_weight, preferred_element_type=f32).astype(bf16)
    return (projected, centroids[None])


def solution(mesh):
    in_specs = (
        P("head", "ctx", None),
        P("head", "ctx", None),
        P("head", "ctx", None),
        P("head", "ctx", None),
        P(None, "head"),
    )
    out_specs = (P("ctx", "head"), P("head", "ctx", None))
    body = functools.partial(shards, mesh.shape["ctx"], mesh.shape["head"])
    return jax.shard_map(body, mesh=mesh, in_specs=in_specs, out_specs=out_specs, check_vma=False)
```

```python
import functools

import jax
import jax.numpy as jnp
from jax import lax
from jax.experimental import pallas as pl
from jax.experimental.pallas import tpu as pltpu
from jax.sharding import PartitionSpec as P

CL_DEV = 2
CAP = 1024
EMPTY = 2.0**100
LOW = -1e30

norm_eps = 1e-06
MESH = pl.DeviceIdType.MESH


def dot_t(a, b):
    return lax.dot_general(a, b, (((1,), (1,)), ((), ())), preferred_element_type=jnp.float32)


def unit_rows(values):
    return values * lax.rsqrt(jnp.mean(values * values, axis=-1, keepdims=True) + norm_eps)


def slots_of(ids, clusters, send):
    tokens = ids.shape[1]
    step = min(256, tokens)
    names = lax.broadcasted_iota(jnp.int32, (clusters, step), 0)
    before = lax.broadcasted_iota(jnp.int32, (step, step), 0)
    after = lax.broadcasted_iota(jnp.int32, (step, step), 1)
    earlier = jnp.where(before < after, 1.0, 0.0).astype(jnp.bfloat16)
    carry = jnp.zeros((clusters, 1), jnp.float32)
    out = []
    for start in range(0, tokens, step):
        part = ids[:, start : start + step]
        named = jnp.where(names == part, 1.0, 0.0)
        count = jnp.dot(named.astype(jnp.bfloat16), earlier, preferred_element_type=jnp.float32)
        rank = jnp.sum(named * (count + carry), axis=0, keepdims=True)
        carry = carry + jnp.sum(named, axis=1, keepdims=True)
        out.append(part * send + rank.astype(jnp.int32))
    return jnp.concatenate(out, axis=1)


def kernel(n, heads, send, q_hbm, k_hbm, v_hbm, ids_ref, joined_ref, cent_ref,
           rows, msg, recv, att, back, keys, bias, in_sem, f_send, f_recv, b_send, b_recv, h_send, h_recv):
    tokens, width = q_hbm.shape[1], q_hbm.shape[2]
    pack = CL_DEV * send
    clusters = CL_DEV * n
    me = lax.axis_index("ctx")
    head = lax.axis_index("head")

    loads = []
    for i, ref in enumerate((q_hbm, k_hbm, v_hbm)):
        load = pltpu.make_async_copy(ref.at[0], rows.at[:, i * width : (i + 1) * width], in_sem.at[i])
        load.start()
        loads.append(load)

    barrier = pltpu.get_barrier_semaphore()

    def greet(i, carry):
        pl.semaphore_signal(barrier, inc=1, device_id=(lax.rem(me + i, n), head), device_id_type=MESH)
        return carry

    lax.fori_loop(1, n, greet, 0)
    for i in range(1, heads):
        pl.semaphore_signal(barrier, inc=1, device_id=(me, lax.rem(head + i, heads)), device_id_type=MESH)

    slot_row = slots_of(ids_ref[...], clusters, send)
    slot_col = jnp.transpose(jnp.broadcast_to(slot_row, (128, tokens)))
    rows[:, 3 * width :] = jnp.ones((tokens, width), jnp.bfloat16)
    for load in loads:
        load.wait()

    chunk = max(128, pack)
    peers = chunk // pack
    chunks = n // peers
    chunk_iota = lax.broadcasted_iota(jnp.int32, (chunk, tokens), 0)
    mine = me // peers

    def fill(c):
        place = jnp.where(chunk_iota + c * chunk == slot_row, 1.0, 0.0).astype(jnp.bfloat16)
        placed = jnp.dot(place, rows[...], preferred_element_type=jnp.float32)
        held = placed[:, 3 * width :]
        part = jnp.concatenate(
            [
                placed[:, :width],
                jnp.where(held > 0.5, placed[:, width : 2 * width], EMPTY),
                placed[:, 2 * width : 3 * width],
            ],
            axis=1,
        ).astype(jnp.bfloat16)
        msg[pl.ds(c * peers, peers)] = part.reshape(peers, pack, 3 * width)

    def forward(d):
        return pltpu.make_async_remote_copy(
            src_ref=msg.at[d], dst_ref=recv.at[me], send_sem=f_send.at[d], recv_sem=f_recv.at[me],
            device_id=(d, head), device_id_type=MESH)

    def ship(c):
        for i in range(peers):
            d = c * peers + i

            @pl.when(d != me)
            def _():
                forward(d).start()

    quarter = chunks // 4

    def order(i):
        turn = lax.rem(i + 1, chunks)
        return lax.rem(mine // quarter + turn // quarter, 4) * quarter + lax.rem(mine + turn, quarter)

    fill(order(0))
    pl.semaphore_wait(barrier, n - 1 + heads - 1)

    def dispatch(i, carry):
        fill(order(i))
        ship(order(i - 1))
        return carry

    lax.fori_loop(1, chunks, dispatch, 0)
    ship(order(chunks - 1))
    recv[me] = msg[me]

    def arrived(s):
        @pl.when(s != me)
        def _():
            pltpu.make_async_remote_copy(
                src_ref=msg.at[s], dst_ref=recv.at[s], send_sem=f_send.at[s], recv_sem=f_recv.at[s],
                device_id=(me, head), device_id_type=MESH).wait_recv()

    def returned(s):
        return pltpu.make_async_remote_copy(
            src_ref=att.at[s], dst_ref=back.at[me], send_sem=b_send.at[s], recv_sem=b_recv.at[me],
            device_id=(s, head), device_id_type=MESH)

    block = 256
    sources = block // send
    tri_r = lax.broadcasted_iota(jnp.int32, (block, block), 0)
    tri_c = lax.broadcasted_iota(jnp.int32, (block, block), 1)
    causal = jnp.where(tri_c <= tri_r, 0.0, LOW)
    ones = jnp.ones((8, width), jnp.bfloat16)
    sums = [jnp.zeros((1, width), jnp.float32) for _ in range(CL_DEV)]
    scale = jnp.float32(width ** (-0.5))

    for b in range(CAP // block):
        first, last = b * sources, (b + 1) * sources

        def wait_one(s, carry):
            arrived(s)
            return carry

        lax.fori_loop(first, last, wait_one, 0)
        span = (b + 1) * block
        for j in range(CL_DEV):
            inner = slice(j * send, (j + 1) * send)
            q = recv[first:last, inner, :width].reshape(block, width)
            k32 = recv[first:last, inner, width : 2 * width].reshape(block, width).astype(jnp.float32)
            vacant = k32 > 0.5 * EMPTY
            k32 = jnp.where(vacant, 0.0, k32)
            keys[j, b * block : span, :] = k32.astype(jnp.bfloat16)
            flags = dot_t(ones, jnp.where(vacant, 1.0, 0.0).astype(jnp.bfloat16))
            bias[j, :, b * block : span] = jnp.where(flags > 0.5, LOW, 0.0)
            unit = unit_rows(q.astype(jnp.float32)) + unit_rows(k32)
            sums[j] = sums[j] + jnp.sum(unit, axis=0, keepdims=True)
            scores = dot_t(q, keys[j, :span, :]) * scale + bias[j, 0:1, :span]
            tail = scores[:, b * block :] + causal
            scores = tail if b == 0 else jnp.concatenate([scores[:, : b * block], tail], axis=1)
            highest = jnp.max(scores, axis=1, keepdims=True)
            weights = jnp.exp(scores - highest)
            total = jnp.sum(weights, axis=1, keepdims=True)
            v = recv[:last, inner, 2 * width :].reshape(span, width)
            mixed = jnp.dot(weights.astype(jnp.bfloat16), v, preferred_element_type=jnp.float32)
            att[first:last, inner, :] = (mixed / total).astype(jnp.bfloat16).reshape(sources, send, width)

        def give_one(s, carry):
            @pl.when(s != me)
            def _():
                returned(s).start()

            return carry

        lax.fori_loop(first, last, give_one, 0)

    for j in range(CL_DEV):
        mean = jnp.mean(sums[j] * sums[j], axis=-1, keepdims=True)
        cent_ref[j : j + 1, :] = sums[j] * lax.rsqrt(mean + norm_eps)
    back[me] = att[me]

    slots = CL_DEV * CAP
    step = 256
    group = step // pack
    lanes = lax.broadcasted_iota(jnp.int32, (tokens, 128), 1)
    got = jnp.zeros((tokens, width), jnp.float32)
    for c in range(slots // step):

        def wait_back(s, carry):
            @pl.when(s != me)
            def _():
                pltpu.make_async_remote_copy(
                    src_ref=att.at[s], dst_ref=back.at[s], send_sem=b_send.at[s], recv_sem=b_recv.at[s],
                    device_id=(me, head), device_id_type=MESH).wait_recv()

            return carry

        lax.fori_loop(c * group, (c + 1) * group, wait_back, 0)
        pick = jnp.concatenate(
            [jnp.where(slot_col == lanes + (c * step + i), 1.0, 0.0) for i in range(0, step, 128)], axis=1
        ).astype(jnp.bfloat16)
        piece = back[c * group : (c + 1) * group].reshape(step, width)
        got = got + jnp.dot(pick, piece, preferred_element_type=jnp.float32)

    own = pl.ds(pl.multiple_of(head * width, width), width)
    joined_ref[:, own] = got.astype(jnp.bfloat16)

    def share(i):
        return pltpu.make_async_remote_copy(
            src_ref=joined_ref.at[:, own], dst_ref=joined_ref.at[:, own],
            send_sem=h_send.at[i - 1], recv_sem=h_recv.at[i - 1],
            device_id=(me, lax.rem(head + i, heads)), device_id_type=MESH)

    for i in range(1, heads):
        share(i).start()

    def sent(i, carry):
        d = lax.rem(me + i, n)
        forward(d).wait_send()
        returned(d).wait_send()
        return carry

    lax.fori_loop(1, n, sent, 0)
    for i in range(1, heads):
        share(i).wait_send()
        other = pl.ds(pl.multiple_of(lax.rem(head + heads - i, heads) * width, width), width)
        pltpu.make_async_remote_copy(
            src_ref=joined_ref.at[:, other], dst_ref=joined_ref.at[:, other],
            send_sem=h_send.at[i - 1], recv_sem=h_recv.at[i - 1],
            device_id=(me, head), device_id_type=MESH).wait_recv()


def shards(n, heads, queries, key_rows, value_rows, cluster_ids, out_weight):
    tokens, width = queries.shape[1], queries.shape[2]
    send = CAP // n
    pack = CL_DEV * send
    bf16, f32 = jnp.bfloat16, jnp.float32
    dma = pltpu.SemaphoreType.DMA
    joined, centroids = pl.pallas_call(
        functools.partial(kernel, n, heads, send),
        out_shape=(
            jax.ShapeDtypeStruct((tokens, heads * width), bf16),
            jax.ShapeDtypeStruct((CL_DEV, width), f32),
        ),
        in_specs=[pl.BlockSpec(memory_space=pl.ANY)] * 3 + [pl.BlockSpec(memory_space=pltpu.VMEM)],
        out_specs=(pl.BlockSpec(memory_space=pltpu.VMEM), pl.BlockSpec(memory_space=pltpu.VMEM)),
        scratch_shapes=[
            pltpu.VMEM((tokens, 4 * width), bf16),
            pltpu.VMEM((n, pack, 3 * width), bf16),
            pltpu.VMEM((n, pack, 3 * width), bf16),
            pltpu.VMEM((n, pack, width), bf16),
            pltpu.VMEM((n, pack, width), bf16),
            pltpu.VMEM((CL_DEV, CAP, width), bf16),
            pltpu.VMEM((CL_DEV, 8, CAP), f32),
            dma((3,)),
            dma((n,)),
            dma((n,)),
            dma((n,)),
            dma((n,)),
            dma((max(1, heads - 1),)),
            dma((max(1, heads - 1),)),
        ],
        compiler_params=pltpu.CompilerParams(
            collective_id=0, has_side_effects=True, vmem_limit_bytes=60000000
        ),
        name="route",
    )(queries, key_rows, value_rows, cluster_ids[0, :, 0][None, :])
    projected = jnp.dot(joined, out_weight, preferred_element_type=f32).astype(bf16)
    return (projected, centroids[None])


def solution(mesh):
    in_specs = (
        P("head", "ctx", None),
        P("head", "ctx", None),
        P("head", "ctx", None),
        P("head", "ctx", None),
        P(None, "head"),
    )
    out_specs = (P("ctx", "head"), P("head", "ctx", None))
    body = functools.partial(shards, mesh.shape["ctx"], mesh.shape["head"])
    return jax.shard_map(body, mesh=mesh, in_specs=in_specs, out_specs=out_specs, check_vma=False)
```
